32 devices in a mesh: samp: 8 (over z, x), state: 4 (over y, core).
Axes of the slice: x: 2, y: 2, z: 4, core: 2. Of those that a mesh axis runs over, the one named last changes fastest.
Arguments:
- energies: bfloat16 [4096, 131072], P('state', 'samp'), may hold values from -12 to 12
- offsets: float32 [4096, 1024], P('state', 'samp'), may hold values from -250 to 250
- counts: int32 [4096], P('state'), may hold values from 1 to 31745, as said below
- labels: int32 [131072], P('samp'), may hold values from 0 to 4095
Outputs:
- free_energy: float32 [4096], P('state')
- own_log_probability: float32 [131072], P('samp')
The draws below stay inside these ranges and needn't reach their ends.
Inputs may be any that keep to these rules, and one draw needn't show every extreme that they name: counts[k] is the number of samples n with labels[n] = k; every state has a sample, state 4096 - 1 has exactly one, and state 0 has the most.
All inputs are finite; a program needn't handle non-finite values.
Results may differ from the reference program's by a relative error of at most 0.0003.
Values sent between devices are 32-bit elements; how exact they have to be, the bound alone decides.
A program may use at most 256 MiB of HBM per device.

```python
import jax
import jax.numpy as jnp
from jax import lax

STATES = 4096
BLOCK = 128
ITERS = 3
SAMPLES = 131072


def labels_and_counts(key):
    base = jax.random.fold_in(key, 4711)
    first, second, third = jax.random.split(base, 3)
    extra = SAMPLES - STATES
    reserved = extra // 4
    picks = jnp.minimum(jax.random.randint(first, (extra,), 1, STATES - 1), jax.random.randint(second, (extra,), 1, STATES - 1))
    picks = jnp.where(jnp.arange(extra, dtype=jnp.int32) < reserved, 0, picks).astype(jnp.int32)
    allof = jnp.concatenate([jnp.arange(STATES, dtype=jnp.int32), picks])
    order = jax.random.permutation(third, SAMPLES)
    labels = allof[order].astype(jnp.int32)
    counts = jax.ops.segment_sum(jnp.ones((SAMPLES,), jnp.int32), labels, num_segments=STATES)
    return (labels, counts.astype(jnp.int32))


def draw_labels(key, part):
    return labels_and_counts(key)[0]


def draw_counts(key, part):
    return labels_and_counts(key)[1]


def draw_offsets(key, part):
    first = jax.random.fold_in(jax.random.fold_in(key, 99), 0)
    nblk = SAMPLES // BLOCK
    rough = 2.0 * jnp.clip(jax.random.normal(first, (STATES, nblk), jnp.float32), -6.0, 6.0)
    return rough


def levels(key, shape, cuts, smallest, largest):
    level, own = 1.0, jax.random.fold_in(key, 6)
    for dim, blocks in cuts:
        steps = jnp.exp(jax.random.uniform(jax.random.fold_in(own, dim), (blocks,), jnp.float32, smallest / len(cuts), largest / len(cuts)))
        level = level * jnp.repeat(steps, shape[dim] // blocks).reshape([-1 if axis == dim else 1 for axis in range(len(shape))])
    return level


def noise(rng, dims, scale, reach, pieces=(), kind=jnp.bfloat16):
    level = levels(rng, dims, pieces, -0.22, 0.18) if pieces else 1.0
    entries = jax.random.normal(rng, dims, jnp.float32) * scale * level
    return jnp.minimum(jnp.maximum(entries, -reach), reach).astype(kind)


def setup_inputs(seed: int = 0) -> dict:
    streams_of = jax.random.split(jax.random.key(seed), 5)
    return {
        "energies": noise(streams_of[0], (STATES, SAMPLES), 2.0, 12.0, ((0, 4), (1, 8))),
        "offsets": draw_offsets(jax.random.fold_in(streams_of[4], 71), 0),
        "counts": draw_counts(jax.random.fold_in(streams_of[4], 71), 0),
        "labels": draw_labels(jax.random.fold_in(streams_of[4], 71), 0),
    }


def energy_rows(energies, offsets, start, rows):
    part = lax.dynamic_slice_in_dim(energies, start, rows, 0).astype(jnp.float32)
    shift = lax.dynamic_slice_in_dim(offsets, start, rows, 0)
    nblk = offsets.shape[1]
    return (part.reshape(rows, nblk, BLOCK) + shift[:, :, None]).reshape(rows, nblk * BLOCK)


def denominator(energies, offsets, logc, free):
    rows = min(256, STATES)
    count = STATES // rows

    def step(carry, index):
        best, total = carry
        start = (index * rows).astype(jnp.int32)
        u = energy_rows(energies, offsets, start, rows)
        lead = lax.dynamic_slice_in_dim(logc + free, start, rows, 0)
        terms = lead[:, None] - u
        newbest = jnp.maximum(best, jnp.max(terms, axis=0))
        total = total * jnp.exp(best - newbest) + jnp.sum(jnp.exp(terms - newbest[None, :]), axis=0)
        return (newbest, total), None

    init = (jnp.full((SAMPLES,), -1e30, jnp.float32), jnp.zeros((SAMPLES,), jnp.float32))
    (best, total), _ = lax.scan(step, init, jnp.arange(count, dtype=jnp.int32))
    return best + jnp.log(total)


def update(energies, offsets, denom):
    rows = min(256, STATES)
    count = STATES // rows

    def one(index):
        start = (index * rows).astype(jnp.int32)
        terms = -energy_rows(energies, offsets, start, rows) - denom[None, :]
        best = jnp.max(terms, axis=1)
        return -(best + jnp.log(jnp.sum(jnp.exp(terms - best[:, None]), axis=1)))

    return lax.map(one, jnp.arange(count, dtype=jnp.int32)).reshape(STATES)


def reference(energies, offsets, counts, labels):
    logc = jnp.log(counts.astype(jnp.float32))
    free = jnp.zeros((STATES,), jnp.float32)
    for step in range(ITERS):
        denom = denominator(energies, offsets, logc, free)
        free = update(energies, offsets, denom)
    denom = denominator(energies, offsets, logc, free)
    picked = jnp.take_along_axis(energies, labels[None, :], axis=0)[0].astype(jnp.float32)
    blocks = (jnp.arange(SAMPLES, dtype=jnp.int32) // BLOCK).astype(jnp.int32)
    picked = picked + offsets[labels, blocks]
    own = logc[labels] + free[labels] - picked - denom
    return free - free[0], own
```

```python
import functools

import jax
import jax.numpy as jnp
from jax import lax
from jax.experimental import pallas as pl
from jax.experimental.pallas import tpu as pltpu
from jax.sharding import PartitionSpec as P

ITERS = 3
AHEAD = 4
SUB = 8
LANE = 128
NLOG2E = -1.4426950408889634
NT = (((1,), (1,)), ((), ()))


def kernel(ns, np_, nc, nh, eng, off_h, cnt_h, lab_h, free_o, own_o, E, ET, off, cnt, lab, offT, pick, dbuf, obuf, fbuf, abuf, lead_s,
           free_s, m_s, s_s, T, d_s, low_s, part_s, in_sem, load_sem, dss, drs, oss, ors, fss, frs, ass, ars):
    rows = E.shape[2]
    half = rows // nh
    nt = ET.shape[1] * LANE
    nm, nv = m_s.shape[1], half - m_s.shape[1]
    gw = SUB * LANE
    groups = E.shape[0]
    per = groups // nc
    st = lax.axis_index("state")
    sp = lax.axis_index("samp")

    def load(g, i):
        return pltpu.make_async_copy(eng.at[:, pl.ds(pl.multiple_of(g * gw + i * LANE, LANE), LANE)], E.at[g, i],
                                     load_sem.at[g, i])

    small = [pltpu.make_async_copy(src, dst, in_sem.at[i])
             for i, (src, dst) in enumerate(((off_h, off), (cnt_h, cnt), (lab_h, lab)))]
    for copy in small:
        copy.start()

    def load_group(g):
        for i in range(SUB):
            load(g, i).start()

    @pl.loop(0, AHEAD)
    def _(g):
        load_group(g)

    barrier = pltpu.get_barrier_semaphore()
    for s in range(1, ns):
        pl.semaphore_signal(barrier, inc=1, device_id={"state": lax.rem(st + s, ns)})
    for s in range(1, np_):
        pl.semaphore_signal(barrier, inc=1, device_id={"samp": lax.rem(sp + s, np_)})

    for copy in small:
        copy.wait()
    offT[...] = off[...].T.reshape(groups, SUB, rows)
    logc = jnp.log(cnt[...].astype(jnp.float32))
    lead_s[...] = logc
    T[...] = jnp.zeros(T.shape, jnp.float32)

    rowid = lax.broadcasted_iota(jnp.int32, (SUB, LANE), 0)

    def split(x):
        hi = x.astype(jnp.bfloat16)
        lo = (x - hi.astype(jnp.float32)).astype(jnp.bfloat16)
        return jnp.concatenate([hi, lo], axis=0)

    def dcopy(it, c, s):
        part = dbuf.at[it, st, pl.ds(c * per, per)]
        return pltpu.make_async_remote_copy(
            part, part, dss.at[it, c, s - 1], drs.at[it, c, s - 1], device_id={"state": lax.rem(st + s, ns)})

    def ocopy(c, s):
        part = obuf.at[st, pl.ds(c * per, per)]
        return pltpu.make_async_remote_copy(
            part, part, oss.at[c, s - 1], ors.at[c, s - 1], device_id={"state": lax.rem(st + s, ns)})

    def weights(g, sl=slice(None)):
        a = lead_s[:, sl] - offT[g, :, sl]
        top = jnp.max(a, axis=1, keepdims=True)
        return a, top, split(jnp.exp(a - top))

    def place(tot, c, out):
        out = out[:SUB] + out[SUB:]
        tot = jnp.where(rowid == 2 * c, out[:, :LANE], tot)
        return jnp.where(rowid == 2 * c + 1, out[:, LANE:], tot)

    def logadd(x, y):
        top = jnp.maximum(x, y)
        return top + jnp.log(jnp.exp(x - top) + jnp.exp(y - top))

    def denom_group(it, g, h, last):
        sl = slice(h * half, (h + 1) * half)
        a, top, w = weights(g, sl)
        tot = jnp.zeros((SUB, LANE), jnp.float32)
        for c in range(SUB // 2):
            out = jnp.dot(w, jnp.concatenate([E[g, 2 * c, sl], E[g, 2 * c + 1, sl]], axis=1), preferred_element_type=jnp.float32)
            tot = place(tot, c, out)
        val = top + jnp.log(tot)
        if h:
            val = logadd(part_s[g], val)
        if h < nh - 1:
            part_s[g] = val
        else:
            dbuf[it, st, g] = val
        if last:
            label = lab[g] - st * rows
            low = label & (LANE - 1)
            high = label >> 7
            sel = obuf[st, g] if h else -pick[g]
            for q in range(half // LANE):
                got = jnp.take_along_axis(a[:, q * LANE:(q + 1) * LANE], low, axis=1)
                sel = jnp.where(high == h * (half // LANE) + q, sel + got, sel)
            obuf[st, g] = sel

    def first_group(g):
        @pl.when(g < groups - AHEAD)
        def _():
            load_group(g + AHEAD)

        for i in range(SUB):
            load(g, i).wait()
        _, top, w = weights(g)
        tot = jnp.zeros((SUB, LANE), jnp.float32)
        ids = lax.broadcasted_iota(jnp.int32, (16, LANE), 0)
        for c in range(SUB // 2):
            high, low, acc = [], [], []
            for h in range(2):
                label = jnp.broadcast_to(lab[g, 2 * c + h:2 * c + h + 1, :] - st * rows, (16, LANE))
                high.append((label >> 4).astype(jnp.int16))
                low.append(label & 15)
                acc.append(jnp.zeros((16, LANE), jnp.bfloat16))
            out = jnp.zeros((2 * SUB, 2 * LANE), jnp.float32)
            col = [[], []]
            for k in range(rows // 512):
                tiles = []
                for q in range(k * 32, (k + 1) * 32):
                    pair = []
                    for h in range(2):
                        at = (g, 2 * c + h, slice(q * 16, (q + 1) * 16), slice(None))
                        e = E[at]
                        v = jnp.exp2(e.astype(jnp.float32) * NLOG2E).astype(jnp.bfloat16)
                        E[at] = v
                        pair.append(v)
                        if q * 16 < nt:
                            col[h].append(v)
                            if len(col[h]) == LANE // 16:
                                ET[g, q // (LANE // 16), (2 * c + h) * LANE:(2 * c + h + 1) * LANE, :] = jnp.concatenate(col[h], axis=0).T
                                col[h] = []
                        acc[h] = jnp.where(high[h] == jnp.int16(q), e, acc[h])
                    tiles.append(jnp.concatenate(pair, axis=1))
                out += jnp.dot(w[:, k * 512:(k + 1) * 512], jnp.concatenate(tiles, axis=0),
                               preferred_element_type=jnp.float32)
            for h in range(2):
                got = jnp.where(low[h] == ids, acc[h].astype(jnp.float32), 0.0)
                pick[g, 2 * c + h:2 * c + h + 1, :] = jnp.sum(got, axis=0, keepdims=True)
            tot = place(tot, c, out)
        dbuf[0, st, g] = top + jnp.log(tot)

    @pl.loop(0, nc)
    def _(c):
        @pl.loop(0, per)
        def _(j):
            first_group(c * per + j)

        @pl.when(c == 0)
        def _():
            pl.semaphore_wait(barrier, ns + np_ - 2)

        for s in range(1, ns):
            dcopy(0, c, s).start()

    def denominator(it, h, last):
        @pl.loop(0, nc)
        def _(c):
            for j in range(per):
                denom_group(it, c * per + j, h, last)
            if h == nh - 1:
                for s in range(1, ns):
                    dcopy(it, c, s).start()
                    if last:
                        ocopy(c, s).start()

    def join(it, g):
        vals = [dbuf[it, q, g] for q in range(ns)]
        top = functools.reduce(jnp.maximum, vals)
        return top + jnp.log(sum(jnp.exp(v - top) for v in vals))

    def fcopy(it, h, s):
        return pltpu.make_async_remote_copy(
            fbuf.at[it, h, sp], fbuf.at[it, h, sp], fss.at[it, h, s - 1], frs.at[it, h, s - 1],
            device_id={"samp": lax.rem(sp + s, np_)})

    def update_group(it, g, h):
        if h == 0:
            d = join(it, g)
            low = jnp.min(d, axis=1, keepdims=True)
            d_s[g] = d
            low_s[g] = jnp.broadcast_to(low, (SUB, LANE))
        else:
            d = d_s[g]
            low = low_s[g, :, 0:1]
        r = jnp.exp(low - d)
        base = h * half
        lhs = split(jnp.concatenate([jnp.where(rowid == i, r, 0.0) for i in range(SUB)], axis=1))
        cuts = sorted({*range(0, min(nt, nm), 256), *range(min(nt, nm), nm, 256), nm})
        for q, end in zip(cuts, cuts[1:]):
            sl = slice(q, end)
            at = slice(base + sl.start, base + sl.stop)
            if at.stop <= nt:
                out = jnp.dot(lhs, jnp.concatenate([ET[g, k] for k in range(at.start // LANE, at.stop // LANE)], axis=1),
                              preferred_element_type=jnp.float32)
            else:
                out = lax.dot_general(lhs, jnp.concatenate([E[g, i, at, :] for i in range(SUB)], axis=1), NT,
                                      preferred_element_type=jnp.float32)
            x = jnp.log(out[:SUB] + out[SUB:]) - offT[g, :, at] - low
            m = m_s[:, sl]
            new = jnp.maximum(m, x)
            s_s[:, sl] = s_s[:, sl] * jnp.exp(m - new) + jnp.exp(x - new)
            m_s[:, sl] = new
        wide = [jnp.broadcast_to(r[i:i + 1, :], (16, LANE)) for i in range(SUB)]
        lane = lax.broadcasted_iota(jnp.int32, (16, LANE), 1)
        for t in range(0, nv, 16):
            acc = T[t:t + 16, :]
            at = base + nm + t
            for i in range(SUB):
                v = E[g, i, at:at + 16, :].astype(jnp.float32) * wide[i]
                acc = jnp.where(lane == g * SUB + i, jnp.sum(v, axis=1, keepdims=True), acc)
            T[t:t + 16, :] = acc

    def update(it, h):
        m_s[...] = jnp.full(m_s.shape, -1e30, jnp.float32)
        s_s[...] = jnp.zeros(s_s.shape, jnp.float32)

        @pl.loop(0, nc)
        def _(c):
            if h == 0:
                for s in range(1, ns):
                    dcopy(it, c, s).wait()

            for j in range(per):
                update_group(it, c * per + j, h)

        m = m_s[...]
        top = jnp.max(m, axis=0, keepdims=True)
        fbuf[it, h, sp, :, 0:nm] = top + jnp.log(jnp.sum(s_s[...] * jnp.exp(m - top), axis=0, keepdims=True))
        if nv:
            x = jnp.log(T[...].T).reshape(groups, SUB, nv) - offT[:, :, h * half + nm:(h + 1) * half] - low_s[:, :, 0:1]
            top = jnp.max(x, axis=(0, 1), keepdims=True)
            fbuf[it, h, sp, :, nm:] = (top + jnp.log(jnp.sum(jnp.exp(x - top), axis=(0, 1), keepdims=True)))[0]
        for s in range(1, np_):
            fcopy(it, h, s).start()

    def finish(it, h):
        for s in range(1, np_):
            fcopy(it, h, s).wait()
        vals = [fbuf[it, h, q] for q in range(np_)]
        top = functools.reduce(jnp.maximum, vals)
        free = -(top + jnp.log(sum(jnp.exp(v - top) for v in vals)))
        sl = slice(h * half, (h + 1) * half)
        free_s[:, sl] = free
        lead_s[:, sl] = jnp.log(cnt[:, sl].astype(jnp.float32)) + free

    def acopy(s):
        return pltpu.make_async_remote_copy(
            abuf.at[st], abuf.at[st], ass.at[s - 1], ars.at[s - 1], device_id={"state": lax.rem(st + s, ns)})

    for it in range(ITERS):
        last = it == ITERS - 1
        for h in range(nh):
            update(it, h)
        for h in range(nh):
            finish(it, h)
            if last and h == 0:
                abuf[st] = free_s[:, :LANE]
                for s in range(1, ns):
                    acopy(s).start()
            denominator(it + 1, h, last)
    for s in range(1, ns):
        acopy(s).wait()
    free_o[...] = free_s[...] - abuf[0][:, 0:1]

    @pl.loop(0, nc)
    def _(c):
        for s in range(1, ns):
            dcopy(ITERS, c, s).wait()
            ocopy(c, s).wait()

        @pl.loop(0, per)
        def _(j):
            g = c * per + j
            own_o[g] = sum(obuf[q, g] for q in range(ns)) - join(ITERS, g)


def solution(mesh):
    ns, np_ = mesh.shape["state"], mesh.shape["samp"]

    def shards(energies, offsets, counts, labels):
        rows, width = energies.shape
        nblk = offsets.shape[1]
        groups = nblk // SUB
        nc = 4
        nh = 1
        gw = width // groups
        nt = rows * 3 // 4
        nv = rows * 3 // 16 if nblk == LANE else 0
        dma = pltpu.SemaphoreType.DMA
        vm = pl.BlockSpec(memory_space=pltpu.VMEM)
        free, own = pl.pallas_call(
            functools.partial(kernel, ns, np_, nc, nh),
            out_shape=(
                jax.ShapeDtypeStruct((1, rows), jnp.float32),
                jax.ShapeDtypeStruct((groups, SUB, LANE), jnp.float32),
            ),
            in_specs=[pl.BlockSpec(memory_space=pl.ANY)] * 4,
            out_specs=(vm, vm),
            scratch_shapes=[
                pltpu.VMEM((groups, SUB, rows, LANE), jnp.bfloat16),
                pltpu.VMEM((groups, nt // LANE, gw, LANE), jnp.bfloat16),
                pltpu.VMEM(offsets.shape, jnp.float32),
                pltpu.VMEM((1, rows), jnp.int32),
                pltpu.VMEM((groups, SUB, LANE), jnp.int32),
                pltpu.VMEM((groups, SUB, rows), jnp.float32),
                pltpu.VMEM((groups, SUB, LANE), jnp.float32),
                pltpu.VMEM((ITERS + 1, ns, groups, SUB, LANE), jnp.float32),
                pltpu.VMEM((ns, groups, SUB, LANE), jnp.float32),
                pltpu.VMEM((ITERS, nh, np_, 1, rows // nh), jnp.float32),
                pltpu.VMEM((ns, 1, LANE), jnp.float32),
                pltpu.VMEM((1, rows), jnp.float32),
                pltpu.VMEM((1, rows), jnp.float32),
                pltpu.VMEM((SUB, rows // nh - nv), jnp.float32),
                pltpu.VMEM((SUB, rows // nh - nv), jnp.float32),
                pltpu.VMEM((max(nv, 16), LANE), jnp.float32),
                pltpu.VMEM((groups, SUB, LANE), jnp.float32),
                pltpu.VMEM((groups, SUB, LANE), jnp.float32),
                pltpu.VMEM((groups, SUB, LANE), jnp.float32),
                dma((3,)),
                dma((groups, SUB)),
                dma((ITERS + 1, nc, ns - 1)), dma((ITERS + 1, nc, ns - 1)),
                dma((nc, ns - 1)), dma((nc, ns - 1)),
                dma((ITERS, nh, np_ - 1)), dma((ITERS, nh, np_ - 1)),
                dma((ns - 1,)), dma((ns - 1,)),
            ],
            compiler_params=pltpu.CompilerParams(
                collective_id=0, has_side_effects=True, vmem_limit_bytes=60 * 1024 * 1024),
            name="mbar",
        )(energies, offsets, counts.reshape(1, rows), labels.reshape(groups, SUB, LANE))
        return free.reshape(rows), own.reshape(width)

    return jax.shard_map(
        shards,
        mesh=mesh,
        in_specs=(P("state", "samp"), P("state", "samp"), P("state"), P("samp")),
        out_specs=(P("state"), P("samp")),
        check_vma=False,
    )
```

```python
import functools

import jax
import jax.numpy as jnp
from jax import lax
from jax.experimental import pallas as pl
from jax.experimental.pallas import tpu as pltpu
from jax.sharding import PartitionSpec as P

ITERS = 3
AHEAD = 4
NC = 4
DSTEP = 4
USTEP = 4
SUB = 8
LANE = 128
NLOG2E = -1.4426950408889634
NT = (((1,), (1,)), ((), ()))


def kernel(ns, np_, nc, nh, eng, off_h, cnt_h, lab_h, free_o, own_o, E, ET, off, cnt, lab, offT, pick, dbuf, lbuf, fbuf, abuf, lead_s,
           free_s, m_s, s_s, T, d_s, low_s, part_s, in_sem, load_sem, dss, drs, oss, ors, fss, frs, ass, ars):
    rows = E.shape[2]
    half = rows // nh
    nt = ET.shape[1] * LANE
    nm, nv = m_s.shape[1], half - m_s.shape[1]
    gw = SUB * LANE
    groups = E.shape[0]
    per = groups // nc
    st = lax.axis_index("state")
    sp = lax.axis_index("samp")

    def load(g, i):
        return pltpu.make_async_copy(eng.at[:, pl.ds(pl.multiple_of(g * gw + i * LANE, LANE), LANE)], E.at[g, i],
                                     load_sem.at[g, i])

    small = [pltpu.make_async_copy(src, dst, in_sem.at[i])
             for i, (src, dst) in enumerate(((off_h, off), (cnt_h, cnt), (lab_h, lab)))]
    for copy in small:
        copy.start()

    def load_group(g):
        for i in range(SUB):
            load(g, i).start()

    @pl.loop(0, AHEAD)
    def _(g):
        load_group(g)

    barrier = pltpu.get_barrier_semaphore()
    for s in range(1, ns):
        pl.semaphore_signal(barrier, inc=1, device_id={"state": lax.rem(st + s, ns)})
    for s in range(1, np_):
        pl.semaphore_signal(barrier, inc=1, device_id={"samp": lax.rem(sp + s, np_)})

    for copy in small:
        copy.wait()
    offT[...] = off[...].T.reshape(groups, SUB, rows)
    logc = jnp.log(cnt[...].astype(jnp.float32))
    lead_s[...] = logc
    T[...] = jnp.zeros(T.shape, jnp.float32)

    rowid = lax.broadcasted_iota(jnp.int32, (SUB, LANE), 0)

    def split(x):
        hi = x.astype(jnp.bfloat16)
        lo = (x - hi.astype(jnp.float32)).astype(jnp.bfloat16)
        return jnp.concatenate([hi, lo], axis=0)

    def dcopy(it, c, s):
        part = dbuf.at[it, st, pl.ds(c * per, per)]
        return pltpu.make_async_remote_copy(
            part, part, dss.at[it, c, s - 1], drs.at[it, c, s - 1], device_id={"state": lax.rem(st + s, ns)})

    def lcopy(c, s):
        part = lbuf.at[st, c]
        return pltpu.make_async_remote_copy(
            part, part, oss.at[c, s - 1], ors.at[c, s - 1], device_id={"state": lax.rem(st + s, ns)})

    def weights(g, sl=slice(None)):
        a = lead_s[:, sl] - offT[g, :, sl]
        top = jnp.max(a, axis=1, keepdims=True)
        return a, top, split(jnp.exp(a - top))

    def place(tot, c, out):
        out = out[:SUB] + out[SUB:]
        tot = jnp.where(rowid == 2 * c, out[:, :LANE], tot)
        return jnp.where(rowid == 2 * c + 1, out[:, LANE:], tot)

    def logadd(x, y):
        top = jnp.maximum(x, y)
        return top + jnp.log(jnp.exp(x - top) + jnp.exp(y - top))

    def denom_group(it, g, h, last):
        sl = slice(h * half, (h + 1) * half)
        a, top, w = weights(g, sl)
        tot = jnp.zeros((SUB, LANE), jnp.float32)
        for c in range(SUB // 2):
            out = jnp.dot(w, jnp.concatenate([E[g, 2 * c, sl], E[g, 2 * c + 1, sl]], axis=1), preferred_element_type=jnp.float32)
            tot = place(tot, c, out)
        val = top + jnp.log(tot)
        if h:
            val = logadd(part_s[g], val)
        if h < nh - 1:
            part_s[g] = val
        else:
            if last:
                lbuf[st, lax.div(g, per), 0, lax.rem(g, per)] = val
            else:
                dbuf[it, st, g] = val
        if last:
            label = lab[g] - st * rows
            low = label & (LANE - 1)
            high = label >> 7
            sel = -pick[g]
            for q in range(half // LANE):
                got = jnp.take_along_axis(a[:, q * LANE:(q + 1) * LANE], low, axis=1)
                sel = jnp.where(high == h * (half // LANE) + q, sel + got, sel)
            lbuf[st, lax.div(g, per), 1, lax.rem(g, per)] = sel

    def first_group(g):
        @pl.when(g < groups - AHEAD)
        def _():
            load_group(g + AHEAD)

        for i in range(SUB):
            load(g, i).wait()
        _, top, w = weights(g)
        tot = jnp.zeros((SUB, LANE), jnp.float32)
        ids = lax.broadcasted_iota(jnp.int32, (16, LANE), 0)
        for c in range(SUB // 2):
            high, low, acc = [], [], []
            for h in range(2):
                label = jnp.broadcast_to(lab[g, 2 * c + h:2 * c + h + 1, :] - st * rows, (16, LANE))
                high.append((label >> 4).astype(jnp.int16))
                low.append(label & 15)
                acc.append(jnp.zeros((16, LANE), jnp.bfloat16))
            out = jnp.zeros((2 * SUB, 2 * LANE), jnp.float32)
            col = [[], []]
            for k in range(rows // 512):
                tiles = []
                for q in range(k * 32, (k + 1) * 32):
                    pair = []
                    for h in range(2):
                        at = (g, 2 * c + h, slice(q * 16, (q + 1) * 16), slice(None))
                        e = E[at]
                        v = jnp.exp2(e.astype(jnp.float32) * NLOG2E).astype(jnp.bfloat16)
                        E[at] = v
                        pair.append(v)
                        if q * 16 < nt:
                            col[h].append(v)
                            if len(col[h]) == LANE // 16:
                                ET[g, q // (LANE // 16), (2 * c + h) * LANE:(2 * c + h + 1) * LANE, :] = jnp.concatenate(col[h], axis=0).T
                                col[h] = []
                        acc[h] = jnp.where(high[h] == jnp.int16(q), e, acc[h])
                    tiles.append(jnp.concatenate(pair, axis=1))
                out += jnp.dot(w[:, k * 512:(k + 1) * 512], jnp.concatenate(tiles, axis=0),
                               preferred_element_type=jnp.float32)
            for h in range(2):
                got = jnp.where(low[h] == ids, acc[h].astype(jnp.float32), 0.0)
                pick[g, 2 * c + h:2 * c + h + 1, :] = jnp.sum(got, axis=0, keepdims=True)
            tot = place(tot, c, out)
        dbuf[0, st, g] = top + jnp.log(tot)

    @pl.loop(0, nc)
    def _(c):
        @pl.loop(0, per)
        def _(j):
            first_group(c * per + j)

        @pl.when(c == 0)
        def _():
            pl.semaphore_wait(barrier, ns + np_ - 2)

        for s in range(1, ns):
            dcopy(0, c, s).start()

    def denominator(it, h, last):
        @pl.loop(0, groups // DSTEP)
        def _(c):
            for j in range(DSTEP):
                denom_group(it, c * DSTEP + j, h, last)
                if (j + 1) % per == 0:
                    chunk = c * (DSTEP // per) + j // per
                    for s in range(1, ns):
                        if last:
                            lcopy(chunk, s).start()
                        else:
                            dcopy(it, chunk, s).start()

    def join(vals):
        top = functools.reduce(jnp.maximum, vals)
        return top + jnp.log(sum(jnp.exp(v - top) for v in vals))

    def fcopy(it, h, s):
        return pltpu.make_async_remote_copy(
            fbuf.at[it, h, sp], fbuf.at[it, h, sp], fss.at[it, h, s - 1], frs.at[it, h, s - 1],
            device_id={"samp": lax.rem(sp + s, np_)})

    def update_group(it, g, h):
        if h == 0:
            d = join([dbuf[it, q, g] for q in range(ns)])
            low = jnp.min(d, axis=1, keepdims=True)
            d_s[g] = d
            low_s[g] = jnp.broadcast_to(low, (SUB, LANE))
        else:
            d = d_s[g]
            low = low_s[g, :, 0:1]
        r = jnp.exp(low - d)
        base = h * half
        lhs = split(jnp.concatenate([jnp.where(rowid == i, r, 0.0) for i in range(SUB)], axis=1))
        cuts = sorted({*range(0, min(nt, nm), 256), *range(min(nt, nm), nm, 256), nm})
        for q, end in zip(cuts, cuts[1:]):
            sl = slice(q, end)
            at = slice(base + sl.start, base + sl.stop)
            if at.stop <= nt:
                out = jnp.dot(lhs, jnp.concatenate([ET[g, k] for k in range(at.start // LANE, at.stop // LANE)], axis=1),
                              preferred_element_type=jnp.float32)
            else:
                out = lax.dot_general(lhs, jnp.concatenate([E[g, i, at, :] for i in range(SUB)], axis=1), NT,
                                      preferred_element_type=jnp.float32)
            x = jnp.log(out[:SUB] + out[SUB:]) - offT[g, :, at] - low
            m = m_s[:, sl]
            new = jnp.maximum(m, x)
            s_s[:, sl] = s_s[:, sl] * jnp.exp(m - new) + jnp.exp(x - new)
            m_s[:, sl] = new
        wide = [jnp.broadcast_to(r[i:i + 1, :], (16, LANE)) for i in range(SUB)]
        lane = lax.broadcasted_iota(jnp.int32, (16, LANE), 1)
        for t in range(0, nv, 16):
            acc = T[t:t + 16, :]
            at = base + nm + t
            for i in range(SUB):
                v = E[g, i, at:at + 16, :].astype(jnp.float32) * wide[i]
                acc = jnp.where(lane == g * SUB + i, jnp.sum(v, axis=1, keepdims=True), acc)
            T[t:t + 16, :] = acc

    def update(it, h):
        m_s[...] = jnp.full(m_s.shape, -1e30, jnp.float32)
        s_s[...] = jnp.zeros(s_s.shape, jnp.float32)

        @pl.loop(0, groups // USTEP)
        def _(c):
            for j in range(USTEP):
                if j % per == 0:
                    for s in range(1, ns):
                        dcopy(it, c * (USTEP // per) + j // per, s).wait()
                update_group(it, c * USTEP + j, h)

        m = m_s[...]
        top = jnp.max(m, axis=0, keepdims=True)
        fbuf[it, h, sp, :, 0:nm] = top + jnp.log(jnp.sum(s_s[...] * jnp.exp(m - top), axis=0, keepdims=True))
        if nv:
            x = jnp.log(T[...].T).reshape(groups, SUB, nv) - offT[:, :, h * half + nm:(h + 1) * half] - low_s[:, :, 0:1]
            top = jnp.max(x, axis=(0, 1), keepdims=True)
            fbuf[it, h, sp, :, nm:] = (top + jnp.log(jnp.sum(jnp.exp(x - top), axis=(0, 1), keepdims=True)))[0]
        for s in range(1, np_):
            fcopy(it, h, s).start()

    def finish(it, h):
        for s in range(1, np_):
            fcopy(it, h, s).wait()
        vals = [fbuf[it, h, q] for q in range(np_)]
        top = functools.reduce(jnp.maximum, vals)
        free = -(top + jnp.log(sum(jnp.exp(v - top) for v in vals)))
        sl = slice(h * half, (h + 1) * half)
        free_s[:, sl] = free
        lead_s[:, sl] = jnp.log(cnt[:, sl].astype(jnp.float32)) + free

    def acopy(s):
        return pltpu.make_async_remote_copy(
            abuf.at[st], abuf.at[st], ass.at[s - 1], ars.at[s - 1], device_id={"state": lax.rem(st + s, ns)})

    for it in range(ITERS):
        last = it == ITERS - 1
        for h in range(nh):
            update(it, h)
        for h in range(nh):
            finish(it, h)
            if last and h == 0:
                abuf[st] = free_s[:, :LANE]
                for s in range(1, ns):
                    acopy(s).start()
            denominator(it + 1, h, last)
    for s in range(1, ns):
        acopy(s).wait()
    free_o[...] = free_s[...] - abuf[0][:, 0:1]

    @pl.loop(0, nc)
    def _(c):
        for s in range(1, ns):
            lcopy(c, s).wait()

        @pl.loop(0, per)
        def _(j):
            g = c * per + j
            own_o[g] = sum(lbuf[q, c, 1, j] for q in range(ns)) - join([lbuf[q, c, 0, j] for q in range(ns)])


def solution(mesh):
    ns, np_ = mesh.shape["state"], mesh.shape["samp"]

    def shards(energies, offsets, counts, labels):
        rows, width = energies.shape
        nblk = offsets.shape[1]
        groups = nblk // SUB
        nc = NC
        nh = 1
        gw = width // groups
        nt = rows * 3 // 4
        nv = rows * 3 // 16 if nblk == LANE else 0
        dma = pltpu.SemaphoreType.DMA
        vm = pl.BlockSpec(memory_space=pltpu.VMEM)
        free, own = pl.pallas_call(
            functools.partial(kernel, ns, np_, nc, nh),
            out_shape=(
                jax.ShapeDtypeStruct((1, rows), jnp.float32),
                jax.ShapeDtypeStruct((groups, SUB, LANE), jnp.float32),
            ),
            in_specs=[pl.BlockSpec(memory_space=pl.ANY)] * 4,
            out_specs=(vm, vm),
            scratch_shapes=[
                pltpu.VMEM((groups, SUB, rows, LANE), jnp.bfloat16),
                pltpu.VMEM((groups, nt // LANE, gw, LANE), jnp.bfloat16),
                pltpu.VMEM(offsets.shape, jnp.float32),
                pltpu.VMEM((1, rows), jnp.int32),
                pltpu.VMEM((groups, SUB, LANE), jnp.int32),
                pltpu.VMEM((groups, SUB, rows), jnp.float32),
                pltpu.VMEM((groups, SUB, LANE), jnp.float32),
                pltpu.VMEM((ITERS, ns, groups, SUB, LANE), jnp.float32),
                pltpu.VMEM((ns, nc, 2, groups // nc, SUB, LANE), jnp.float32),
                pltpu.VMEM((ITERS, nh, np_, 1, rows // nh), jnp.float32),
                pltpu.VMEM((ns, 1, LANE), jnp.float32),
                pltpu.VMEM((1, rows), jnp.float32),
                pltpu.VMEM((1, rows), jnp.float32),
                pltpu.VMEM((SUB, rows // nh - nv), jnp.float32),
                pltpu.VMEM((SUB, rows // nh - nv), jnp.float32),
                pltpu.VMEM((max(nv, 16), LANE), jnp.float32),
                pltpu.VMEM((groups, SUB, LANE), jnp.float32),
                pltpu.VMEM((groups, SUB, LANE), jnp.float32),
                pltpu.VMEM((groups, SUB, LANE), jnp.float32),
                dma((3,)),
                dma((groups, SUB)),
                dma((ITERS, nc, ns - 1)), dma((ITERS, nc, ns - 1)),
                dma((nc, ns - 1)), dma((nc, ns - 1)),
                dma((ITERS, nh, np_ - 1)), dma((ITERS, nh, np_ - 1)),
                dma((ns - 1,)), dma((ns - 1,)),
            ],
            compiler_params=pltpu.CompilerParams(
                collective_id=0, has_side_effects=True, vmem_limit_bytes=60 * 1024 * 1024),
            name="mbar",
        )(energies, offsets, counts.reshape(1, rows), labels.reshape(groups, SUB, LANE))
        def results(free_i, own_i, free_o, own_o):
            free_o[...] = free_i[...]
            own_o[...] = own_i[...]

        return pl.pallas_call(
            results,
            out_shape=(jax.ShapeDtypeStruct((rows,), jnp.float32), jax.ShapeDtypeStruct((width,), jnp.float32)),
            in_specs=[vm, vm],
            out_specs=(vm, vm),
            name="results",
        )(free.reshape(rows), own.reshape(width))

    return jax.shard_map(
        shards,
        mesh=mesh,
        in_specs=(P("state", "samp"), P("state", "samp"), P("state"), P("samp")),
        out_specs=(P("state"), P("samp")),
        check_vma=False,
    )
```

```python
import functools

import jax
import jax.numpy as jnp
from jax import lax
from jax.experimental import pallas as pl
from jax.experimental.pallas import tpu as pltpu
from jax.sharding import PartitionSpec as P

ITERS = 3
AHEAD = 8
KC = 256
FIRST = 1
NC = 4
DSTEP = 4
USTEP = 4
SUB = 8
LANE = 128
NLOG2E = -1.4426950408889634
NT = (((1,), (1,)), ((), ()))


def kernel(ns, np_, nc, nh, eng, off_h, cnt_h, lab_h, free_o, own_o, E, ET, off, cnt, lab, offT, pick, dbuf, lbuf, fbuf, abuf, lead_s,
           free_s, m_s, s_s, T, d_s, low_s, part_s, in_sem, load_sem, dss, drs, oss, ors, fss, frs, ass, ars):
    rows = E.shape[2]
    half = rows // nh
    nt = ET.shape[1] * LANE
    nm, nv = m_s.shape[1], half - m_s.shape[1]
    gw = SUB * LANE
    groups = E.shape[0]
    per = groups // nc
    st = lax.axis_index("state")
    sp = lax.axis_index("samp")

    def load(g, i):
        return pltpu.make_async_copy(eng.at[:, pl.ds(pl.multiple_of(g * gw + i * LANE, LANE), LANE)], E.at[g, i],
                                     load_sem.at[g, i])

    small = [pltpu.make_async_copy(src, dst, in_sem.at[i])
             for i, (src, dst) in enumerate(((off_h, off), (cnt_h, cnt), (lab_h, lab)))]
    for copy in small:
        copy.start()

    def load_group(g):
        for i in range(SUB):
            load(g, i).start()

    @pl.loop(0, AHEAD)
    def _(g):
        load_group(g)

    barrier = pltpu.get_barrier_semaphore()
    for s in range(1, ns):
        pl.semaphore_signal(barrier, inc=1, device_id={"state": lax.rem(st + s, ns)})
    for s in range(1, np_):
        pl.semaphore_signal(barrier, inc=1, device_id={"samp": lax.rem(sp + s, np_)})

    for copy in small:
        copy.wait()
    offT[...] = off[...].T.reshape(groups, SUB, rows)
    logc = jnp.log(cnt[...].astype(jnp.float32))
    lead_s[...] = logc
    T[...] = jnp.zeros(T.shape, jnp.float32)

    rowid = lax.broadcasted_iota(jnp.int32, (SUB, LANE), 0)

    def split(x):
        hi = x.astype(jnp.bfloat16)
        lo = (x - hi.astype(jnp.float32)).astype(jnp.bfloat16)
        return jnp.concatenate([hi, lo], axis=0)

    def dcopy(it, c, s):
        part = dbuf.at[it, st, pl.ds(c * per, per)]
        return pltpu.make_async_remote_copy(
            part, part, dss.at[it, c, s - 1], drs.at[it, c, s - 1], device_id={"state": lax.rem(st + s, ns)})

    def lcopy(c, s):
        part = lbuf.at[st, c]
        return pltpu.make_async_remote_copy(
            part, part, oss.at[c, s - 1], ors.at[c, s - 1], device_id={"state": lax.rem(st + s, ns)})

    def weights(g, sl=slice(None)):
        a = lead_s[:, sl] - offT[g, :, sl]
        top = jnp.max(a, axis=1, keepdims=True)
        return a, top, split(jnp.exp(a - top))

    def place(tot, c, out):
        out = out[:SUB] + out[SUB:]
        tot = jnp.where(rowid == 2 * c, out[:, :LANE], tot)
        return jnp.where(rowid == 2 * c + 1, out[:, LANE:], tot)

    def logadd(x, y):
        top = jnp.maximum(x, y)
        return top + jnp.log(jnp.exp(x - top) + jnp.exp(y - top))

    def denom_group(it, g, h, last):
        sl = slice(h * half, (h + 1) * half)
        a, top, w = weights(g, sl)
        tot = jnp.zeros((SUB, LANE), jnp.float32)
        for c in range(SUB // 2):
            out = jnp.dot(w, jnp.concatenate([E[g, 2 * c, sl], E[g, 2 * c + 1, sl]], axis=1), preferred_element_type=jnp.float32)
            tot = place(tot, c, out)
        val = top + jnp.log(tot)
        if h:
            val = logadd(part_s[g], val)
        if h < nh - 1:
            part_s[g] = val
        else:
            if last:
                lbuf[st, lax.div(g, per), 0, lax.rem(g, per)] = val
            else:
                dbuf[it, st, g] = val
        if last:
            label = lab[g] - st * rows
            low = label & (LANE - 1)
            high = label >> 7
            sel = -pick[g]
            for q in range(half // LANE):
                got = jnp.take_along_axis(a[:, q * LANE:(q + 1) * LANE], low, axis=1)
                sel = jnp.where(high == h * (half // LANE) + q, sel + got, sel)
            lbuf[st, lax.div(g, per), 1, lax.rem(g, per)] = sel

    def arrive(g):
        @pl.when(g < groups - AHEAD)
        def _():
            load_group(g + AHEAD)

        for i in range(SUB):
            load(g, i).wait()

    def first_group(g):
        _, top, w = weights(g)
        tot = jnp.zeros((SUB, LANE), jnp.float32)
        ids = lax.broadcasted_iota(jnp.int32, (16, LANE), 0)
        for c in range(SUB // 2):
            high, low, acc = [], [], []
            for h in range(2):
                label = jnp.broadcast_to(lab[g, 2 * c + h:2 * c + h + 1, :] - st * rows, (16, LANE))
                high.append((label >> 4).astype(jnp.int16))
                low.append(label & 15)
                acc.append(jnp.zeros((16, LANE), jnp.bfloat16))
            out = jnp.zeros((2 * SUB, 2 * LANE), jnp.float32)
            col = [[], []]
            for k in range(rows // KC):
                tiles = []
                for q in range(k * KC // 16, (k + 1) * KC // 16):
                    pair = []
                    for h in range(2):
                        at = (g, 2 * c + h, slice(q * 16, (q + 1) * 16), slice(None))
                        e = E[at]
                        v = jnp.exp2(e.astype(jnp.float32) * NLOG2E).astype(jnp.bfloat16)
                        E[at] = v
                        pair.append(v)
                        if q * 16 < nt:
                            col[h].append(v)
                            if len(col[h]) == LANE // 16:
                                ET[g, q // (LANE // 16), (2 * c + h) * LANE:(2 * c + h + 1) * LANE, :] = jnp.concatenate(col[h], axis=0).T
                                col[h] = []
                        acc[h] = jnp.where(high[h] == jnp.int16(q), e, acc[h])
                    tiles.append(jnp.concatenate(pair, axis=1))
                out += jnp.dot(w[:, k * KC:(k + 1) * KC], jnp.concatenate(tiles, axis=0),
                               preferred_element_type=jnp.float32)
            for h in range(2):
                got = jnp.where(low[h] == ids, acc[h].astype(jnp.float32), 0.0)
                pick[g, 2 * c + h:2 * c + h + 1, :] = jnp.sum(got, axis=0, keepdims=True)
            tot = place(tot, c, out)
        dbuf[0, st, g] = top + jnp.log(tot)

    @pl.loop(0, nc)
    def _(c):
        @pl.loop(0, per // FIRST)
        def _(j):
            for k in range(FIRST):
                arrive(c * per + j * FIRST + k)
            for k in range(FIRST):
                first_group(c * per + j * FIRST + k)

        @pl.when(c == 0)
        def _():
            pl.semaphore_wait(barrier, ns + np_ - 2)

        for s in range(1, ns):
            dcopy(0, c, s).start()

    def denominator(it, h, last):
        @pl.loop(0, groups // DSTEP)
        def _(c):
            for j in range(DSTEP):
                denom_group(it, c * DSTEP + j, h, last)
                if (j + 1) % per == 0:
                    chunk = c * (DSTEP // per) + j // per
                    for s in range(1, ns):
                        if last:
                            lcopy(chunk, s).start()
                        else:
                            dcopy(it, chunk, s).start()

    def join(vals):
        top = functools.reduce(jnp.maximum, vals)
        return top + jnp.log(sum(jnp.exp(v - top) for v in vals))

    def fcopy(it, h, s):
        return pltpu.make_async_remote_copy(
            fbuf.at[it, h, sp], fbuf.at[it, h, sp], fss.at[it, h, s - 1], frs.at[it, h, s - 1],
            device_id={"samp": lax.rem(sp + s, np_)})

    def update_group(it, g, h):
        if h == 0:
            d = join([dbuf[it, q, g] for q in range(ns)])
            low = jnp.min(d, axis=1, keepdims=True)
            d_s[g] = d
            low_s[g] = jnp.broadcast_to(low, (SUB, LANE))
        else:
            d = d_s[g]
            low = low_s[g, :, 0:1]
        r = jnp.exp(low - d)
        base = h * half
        lhs = split(jnp.concatenate([jnp.where(rowid == i, r, 0.0) for i in range(SUB)], axis=1))
        cuts = sorted({*range(0, min(nt, nm), 256), *range(min(nt, nm), nm, 256), nm})
        for q, end in zip(cuts, cuts[1:]):
            sl = slice(q, end)
            at = slice(base + sl.start, base + sl.stop)
            if at.stop <= nt:
                out = jnp.dot(lhs, jnp.concatenate([ET[g, k] for k in range(at.start // LANE, at.stop // LANE)], axis=1),
                              preferred_element_type=jnp.float32)
            else:
                out = lax.dot_general(lhs, jnp.concatenate([E[g, i, at, :] for i in range(SUB)], axis=1), NT,
                                      preferred_element_type=jnp.float32)
            x = jnp.log(out[:SUB] + out[SUB:]) - offT[g, :, at] - low
            m = m_s[:, sl]
            new = jnp.maximum(m, x)
            s_s[:, sl] = s_s[:, sl] * jnp.exp(m - new) + jnp.exp(x - new)
            m_s[:, sl] = new
        wide = [jnp.broadcast_to(r[i:i + 1, :], (16, LANE)) for i in range(SUB)]
        lane = lax.broadcasted_iota(jnp.int32, (16, LANE), 1)
        for t in range(0, nv, 16):
            acc = T[t:t + 16, :]
            at = base + nm + t
            for i in range(SUB):
                v = E[g, i, at:at + 16, :].astype(jnp.float32) * wide[i]
                acc = jnp.where(lane == g * SUB + i, jnp.sum(v, axis=1, keepdims=True), acc)
            T[t:t + 16, :] = acc

    def update(it, h):
        m_s[...] = jnp.full(m_s.shape, -1e30, jnp.float32)
        s_s[...] = jnp.zeros(s_s.shape, jnp.float32)

        @pl.loop(0, groups // USTEP)
        def _(c):
            for j in range(USTEP):
                if j % per == 0:
                    for s in range(1, ns):
                        dcopy(it, c * (USTEP // per) + j // per, s).wait_recv()
                update_group(it, c * USTEP + j, h)

        m = m_s[...]
        top = jnp.max(m, axis=0, keepdims=True)
        fbuf[it, h, sp, :, 0:nm] = top + jnp.log(jnp.sum(s_s[...] * jnp.exp(m - top), axis=0, keepdims=True))
        if nv:
            x = jnp.log(T[...].T).reshape(groups, SUB, nv) - offT[:, :, h * half + nm:(h + 1) * half] - low_s[:, :, 0:1]
            top = jnp.max(x, axis=(0, 1), keepdims=True)
            fbuf[it, h, sp, :, nm:] = (top + jnp.log(jnp.sum(jnp.exp(x - top), axis=(0, 1), keepdims=True)))[0]
        for s in range(1, np_):
            fcopy(it, h, s).start()
        for s in range(1, ns):
            for c in range(nc):
                dcopy(it, c, s).wait_send()
        if it:
            for s in range(1, np_):
                fcopy(it - 1, h, s).wait_send()

    def finish(it, h):
        for s in range(1, np_):
            fcopy(it, h, s).wait_recv()
        vals = [fbuf[it, h, q] for q in range(np_)]
        top = functools.reduce(jnp.maximum, vals)
        free = -(top + jnp.log(sum(jnp.exp(v - top) for v in vals)))
        sl = slice(h * half, (h + 1) * half)
        free_s[:, sl] = free
        lead_s[:, sl] = jnp.log(cnt[:, sl].astype(jnp.float32)) + free

    def acopy(s):
        return pltpu.make_async_remote_copy(
            abuf.at[st], abuf.at[st], ass.at[s - 1], ars.at[s - 1], device_id={"state": lax.rem(st + s, ns)})

    for it in range(ITERS):
        last = it == ITERS - 1
        for h in range(nh):
            update(it, h)
        for h in range(nh):
            finish(it, h)
            if last and h == 0:
                abuf[st] = free_s[:, :LANE]
                for s in range(1, ns):
                    acopy(s).start()
            denominator(it + 1, h, last)
    for s in range(1, ns):
        acopy(s).wait()
    for h in range(nh):
        for s in range(1, np_):
            fcopy(ITERS - 1, h, s).wait_send()
    free_o[...] = free_s[...] - abuf[0][:, 0:1]

    @pl.loop(0, nc)
    def _(c):
        for s in range(1, ns):
            lcopy(c, s).wait()

        @pl.loop(0, per)
        def _(j):
            g = c * per + j
            own_o[g] = sum(lbuf[q, c, 1, j] for q in range(ns)) - join([lbuf[q, c, 0, j] for q in range(ns)])


def solution(mesh):
    ns, np_ = mesh.shape["state"], mesh.shape["samp"]

    def shards(energies, offsets, counts, labels):
        rows, width = energies.shape
        nblk = offsets.shape[1]
        groups = nblk // SUB
        nc = NC
        nh = 1
        gw = width // groups
        nt = rows * 3 // 4
        nv = rows * 7 // 32 if nblk == LANE else 0
        dma = pltpu.SemaphoreType.DMA
        vm = pl.BlockSpec(memory_space=pltpu.VMEM)
        free, own = pl.pallas_call(
            functools.partial(kernel, ns, np_, nc, nh),
            out_shape=(
                jax.ShapeDtypeStruct((1, rows), jnp.float32),
                jax.ShapeDtypeStruct((groups, SUB, LANE), jnp.float32),
            ),
            in_specs=[pl.BlockSpec(memory_space=pl.ANY)] * 4,
            out_specs=(vm, vm),
            scratch_shapes=[
                pltpu.VMEM((groups, SUB, rows, LANE), jnp.bfloat16),
                pltpu.VMEM((groups, nt // LANE, gw, LANE), jnp.bfloat16),
                pltpu.VMEM(offsets.shape, jnp.float32),
                pltpu.VMEM((1, rows), jnp.int32),
                pltpu.VMEM((groups, SUB, LANE), jnp.int32),
                pltpu.VMEM((groups, SUB, rows), jnp.float32),
                pltpu.VMEM((groups, SUB, LANE), jnp.float32),
                pltpu.VMEM((ITERS, ns, groups, SUB, LANE), jnp.float32),
                pltpu.VMEM((ns, nc, 2, groups // nc, SUB, LANE), jnp.float32),
                pltpu.VMEM((ITERS, nh, np_, 1, rows // nh), jnp.float32),
                pltpu.VMEM((ns, 1, LANE), jnp.float32),
                pltpu.VMEM((1, rows), jnp.float32),
                pltpu.VMEM((1, rows), jnp.float32),
                pltpu.VMEM((SUB, rows // nh - nv), jnp.float32),
                pltpu.VMEM((SUB, rows // nh - nv), jnp.float32),
                pltpu.VMEM((max(nv, 16), LANE), jnp.float32),
                pltpu.VMEM((groups, SUB, LANE), jnp.float32),
                pltpu.VMEM((groups, SUB, LANE), jnp.float32),
                pltpu.VMEM((groups, SUB, LANE), jnp.float32),
                dma((3,)),
                dma((groups, SUB)),
                dma((ITERS, nc, ns - 1)), dma((ITERS, nc, ns - 1)),
                dma((nc, ns - 1)), dma((nc, ns - 1)),
                dma((ITERS, nh, np_ - 1)), dma((ITERS, nh, np_ - 1)),
                dma((ns - 1,)), dma((ns - 1,)),
            ],
            compiler_params=pltpu.CompilerParams(
                collective_id=0, has_side_effects=True, vmem_limit_bytes=60 * 1024 * 1024),
            name="mbar",
        )(energies, offsets, counts.reshape(1, rows), labels.reshape(groups, SUB, LANE))
        def results(free_i, own_i, free_o, own_o):
            free_o[...] = free_i[...]
            own_o[...] = own_i[...]

        return pl.pallas_call(
            results,
            out_shape=(jax.ShapeDtypeStruct((rows,), jnp.float32), jax.ShapeDtypeStruct((width,), jnp.float32)),
            in_specs=[vm, vm],
            out_specs=(vm, vm),
            name="results",
        )(free.reshape(rows), own.reshape(width))

    return jax.shard_map(
        shards,
        mesh=mesh,
        in_specs=(P("state", "samp"), P("state", "samp"), P("state"), P("samp")),
        out_specs=(P("state"), P("samp")),
        check_vma=False,
    )
```

```python
import functools

import jax
import jax.numpy as jnp
from jax import lax
from jax.experimental import pallas as pl
from jax.experimental.pallas import tpu as pltpu
from jax.sharding import PartitionSpec as P

ITERS = 3
AHEAD = 8
KC = 256
FIRST = 1
NC = 4
DSTEP = 4
USTEP = 4
SUB = 8
LANE = 128
NLOG2E = -1.4426950408889634
NT = (((1,), (1,)), ((), ()))


def kernel(ns, np_, nc, nh, eng, off_h, cnt_h, lab_h, free_o, own_o, E, ET, off, cnt, lab, offT, pick, dbuf, lbuf, fbuf, abuf, lead_s,
           free_s, m_s, s_s, T, d_s, low_s, part_s, in_sem, load_sem, dss, drs, oss, ors, fss, frs, ass, ars):
    rows = E.shape[2]
    half = rows // nh
    nt = ET.shape[1] * LANE
    nm, nv = m_s.shape[1], half - m_s.shape[1]
    gw = SUB * LANE
    groups = E.shape[0]
    per = groups // nc
    st = lax.axis_index("state")
    sp = lax.axis_index("samp")
    order = sorted(range(1, ns), key=lambda s: -min(s, ns - s))

    def load(g, i):
        return pltpu.make_async_copy(eng.at[:, pl.ds(pl.multiple_of(g * gw + i * LANE, LANE), LANE)], E.at[g, i],
                                     load_sem.at[g, i])

    small = [pltpu.make_async_copy(src, dst, in_sem.at[i])
             for i, (src, dst) in enumerate(((off_h, off), (cnt_h, cnt), (lab_h, lab)))]
    for copy in small:
        copy.start()

    def load_group(g):
        for i in range(SUB):
            load(g, i).start()

    @pl.loop(0, AHEAD)
    def _(g):
        load_group(g)

    barrier = pltpu.get_barrier_semaphore()
    for s in range(1, ns):
        pl.semaphore_signal(barrier, inc=1, device_id={"state": lax.rem(st + s, ns)})
    for s in range(1, np_):
        pl.semaphore_signal(barrier, inc=1, device_id={"samp": lax.rem(sp + s, np_)})

    for copy in small:
        copy.wait()
    offT[...] = off[...].T.reshape(groups, SUB, rows)
    logc = jnp.log(cnt[...].astype(jnp.float32))
    lead_s[...] = logc
    T[...] = jnp.zeros(T.shape, jnp.float32)

    rowid = lax.broadcasted_iota(jnp.int32, (SUB, LANE), 0)

    def split(x):
        hi = x.astype(jnp.bfloat16)
        lo = (x - hi.astype(jnp.float32)).astype(jnp.bfloat16)
        return jnp.concatenate([hi, lo], axis=0)

    def dcopy(it, c, s):
        part = dbuf.at[it, st, pl.ds(c * per, per)]
        return pltpu.make_async_remote_copy(
            part, part, dss.at[it, c, s - 1], drs.at[it, c, s - 1], device_id={"state": lax.rem(st + s, ns)})

    def lcopy(c, s):
        part = lbuf.at[st, c]
        return pltpu.make_async_remote_copy(
            part, part, oss.at[c, s - 1], ors.at[c, s - 1], device_id={"state": lax.rem(st + s, ns)})

    def weights(g, sl=slice(None)):
        a = lead_s[:, sl] - offT[g, :, sl]
        top = jnp.max(a, axis=1, keepdims=True)
        return a, top, split(jnp.exp(a - top))

    def place(tot, c, out):
        out = out[:SUB] + out[SUB:]
        tot = jnp.where(rowid == 2 * c, out[:, :LANE], tot)
        return jnp.where(rowid == 2 * c + 1, out[:, LANE:], tot)

    def logadd(x, y):
        top = jnp.maximum(x, y)
        return top + jnp.log(jnp.exp(x - top) + jnp.exp(y - top))

    def denom_group(it, g, h, last):
        sl = slice(h * half, (h + 1) * half)
        a, top, w = weights(g, sl)
        tot = jnp.zeros((SUB, LANE), jnp.float32)
        for c in range(SUB // 2):
            out = jnp.dot(w, jnp.concatenate([E[g, 2 * c, sl], E[g, 2 * c + 1, sl]], axis=1), preferred_element_type=jnp.float32)
            tot = place(tot, c, out)
        val = top + jnp.log(tot)
        if h:
            val = logadd(part_s[g], val)
        if h < nh - 1:
            part_s[g] = val
        else:
            if last:
                lbuf[st, lax.div(g, per), 0, lax.rem(g, per)] = val
            else:
                dbuf[it, st, g] = val
        if last:
            label = lab[g] - st * rows
            low = label & (LANE - 1)
            high = label >> 7
            sel = -pick[g]
            for q in range(half // LANE):
                got = jnp.take_along_axis(a[:, q * LANE:(q + 1) * LANE], low, axis=1)
                sel = jnp.where(high == h * (half // LANE) + q, sel + got, sel)
            lbuf[st, lax.div(g, per), 1, lax.rem(g, per)] = sel

    def arrive(g):
        @pl.when(g < groups - AHEAD)
        def _():
            load_group(g + AHEAD)

        for i in range(SUB):
            load(g, i).wait()

    def first_group(g):
        _, top, w = weights(g)
        tot = jnp.zeros((SUB, LANE), jnp.float32)
        ids = lax.broadcasted_iota(jnp.int32, (16, LANE), 0)
        for c in range(SUB // 2):
            high, low, acc = [], [], []
            for h in range(2):
                label = jnp.broadcast_to(lab[g, 2 * c + h:2 * c + h + 1, :] - st * rows, (16, LANE))
                high.append((label >> 4).astype(jnp.int16))
                low.append(label & 15)
                acc.append(jnp.zeros((16, LANE), jnp.bfloat16))
            out = jnp.zeros((2 * SUB, 2 * LANE), jnp.float32)
            col = [[], []]
            for k in range(rows // KC):
                tiles = []
                for q in range(k * KC // 16, (k + 1) * KC // 16):
                    pair = []
                    for h in range(2):
                        at = (g, 2 * c + h, slice(q * 16, (q + 1) * 16), slice(None))
                        e = E[at]
                        v = jnp.exp2(e.astype(jnp.float32) * NLOG2E).astype(jnp.bfloat16)
                        E[at] = v
                        pair.append(v)
                        if q * 16 < nt:
                            col[h].append(v)
                            if len(col[h]) == LANE // 16:
                                ET[g, q // (LANE // 16), (2 * c + h) * LANE:(2 * c + h + 1) * LANE, :] = jnp.concatenate(col[h], axis=0).T
                                col[h] = []
                        acc[h] = jnp.where(high[h] == jnp.int16(q), e, acc[h])
                    tiles.append(jnp.concatenate(pair, axis=1))
                out += jnp.dot(w[:, k * KC:(k + 1) * KC], jnp.concatenate(tiles, axis=0),
                               preferred_element_type=jnp.float32)
            for h in range(2):
                got = jnp.where(low[h] == ids, acc[h].astype(jnp.float32), 0.0)
                pick[g, 2 * c + h:2 * c + h + 1, :] = jnp.sum(got, axis=0, keepdims=True)
            tot = place(tot, c, out)
        dbuf[0, st, g] = top + jnp.log(tot)

    @pl.loop(0, nc)
    def _(c):
        @pl.loop(0, per // FIRST)
        def _(j):
            for k in range(FIRST):
                arrive(c * per + j * FIRST + k)
            for k in range(FIRST):
                first_group(c * per + j * FIRST + k)

        @pl.when(c == 0)
        def _():
            pl.semaphore_wait(barrier, ns + np_ - 2)

        for s in order:
            dcopy(0, c, s).start()

    def denominator(it, h, last):
        @pl.loop(0, groups // DSTEP)
        def _(c):
            for j in range(DSTEP):
                denom_group(it, c * DSTEP + j, h, last)
                if (j + 1) % per == 0:
                    chunk = c * (DSTEP // per) + j // per
                    for s in order:
                        if last:
                            lcopy(chunk, s).start()
                        else:
                            dcopy(it, chunk, s).start()

    def join(vals):
        top = functools.reduce(jnp.maximum, vals)
        return top + jnp.log(sum(jnp.exp(v - top) for v in vals))

    def fcopy(it, h, s):
        return pltpu.make_async_remote_copy(
            fbuf.at[it, h, sp], fbuf.at[it, h, sp], fss.at[it, h, s - 1], frs.at[it, h, s - 1],
            device_id={"samp": lax.rem(sp + s, np_)})

    def update_group(it, g, h):
        if h == 0:
            d = join([dbuf[it, q, g] for q in range(ns)])
            low = jnp.min(d, axis=1, keepdims=True)
            d_s[g] = d
            low_s[g] = jnp.broadcast_to(low, (SUB, LANE))
        else:
            d = d_s[g]
            low = low_s[g, :, 0:1]
        r = jnp.exp(low - d)
        base = h * half
        lhs = split(jnp.concatenate([jnp.where(rowid == i, r, 0.0) for i in range(SUB)], axis=1))
        cuts = sorted({*range(0, min(nt, nm), 256), *range(min(nt, nm), nm, 256), nm})
        for q, end in zip(cuts, cuts[1:]):
            sl = slice(q, end)
            at = slice(base + sl.start, base + sl.stop)
            if at.stop <= nt:
                out = jnp.dot(lhs, jnp.concatenate([ET[g, k] for k in range(at.start // LANE, at.stop // LANE)], axis=1),
                              preferred_element_type=jnp.float32)
            else:
                out = lax.dot_general(lhs, jnp.concatenate([E[g, i, at, :] for i in range(SUB)], axis=1), NT,
                                      preferred_element_type=jnp.float32)
            x = jnp.log(out[:SUB] + out[SUB:]) - offT[g, :, at] - low
            m = m_s[:, sl]
            new = jnp.maximum(m, x)
            s_s[:, sl] = s_s[:, sl] * jnp.exp(m - new) + jnp.exp(x - new)
            m_s[:, sl] = new
        wide = [jnp.broadcast_to(r[i:i + 1, :], (16, LANE)) for i in range(SUB)]
        lane = lax.broadcasted_iota(jnp.int32, (16, LANE), 1)
        for t in range(0, nv, 16):
            acc = T[t:t + 16, :]
            at = base + nm + t
            for i in range(SUB):
                v = E[g, i, at:at + 16, :].astype(jnp.float32) * wide[i]
                acc = jnp.where(lane == g * SUB + i, jnp.sum(v, axis=1, keepdims=True), acc)
            T[t:t + 16, :] = acc

    def update(it, h):
        m_s[...] = jnp.full(m_s.shape, -1e30, jnp.float32)
        s_s[...] = jnp.zeros(s_s.shape, jnp.float32)

        @pl.loop(0, groups // USTEP)
        def _(c):
            for j in range(USTEP):
                if j % per == 0:
                    for s in range(1, ns):
                        dcopy(it, c * (USTEP // per) + j // per, s).wait_recv()
                update_group(it, c * USTEP + j, h)

        m = m_s[...]
        top = jnp.max(m, axis=0, keepdims=True)
        fbuf[it, h, sp, :, 0:nm] = top + jnp.log(jnp.sum(s_s[...] * jnp.exp(m - top), axis=0, keepdims=True))
        if nv:
            x = jnp.log(T[...].T).reshape(groups, SUB, nv) - offT[:, :, h * half + nm:(h + 1) * half] - low_s[:, :, 0:1]
            top = jnp.max(x, axis=(0, 1), keepdims=True)
            fbuf[it, h, sp, :, nm:] = (top + jnp.log(jnp.sum(jnp.exp(x - top), axis=(0, 1), keepdims=True)))[0]
        for s in range(1, np_):
            fcopy(it, h, s).start()
        for s in range(1, ns):
            for c in range(nc):
                dcopy(it, c, s).wait_send()
        if it:
            for s in range(1, np_):
                fcopy(it - 1, h, s).wait_send()

    def finish(it, h):
        for s in range(1, np_):
            fcopy(it, h, s).wait_recv()
        vals = [fbuf[it, h, q] for q in range(np_)]
        top = functools.reduce(jnp.maximum, vals)
        free = -(top + jnp.log(sum(jnp.exp(v - top) for v in vals)))
        sl = slice(h * half, (h + 1) * half)
        free_s[:, sl] = free
        lead_s[:, sl] = jnp.log(cnt[:, sl].astype(jnp.float32)) + free

    def acopy(s):
        return pltpu.make_async_remote_copy(
            abuf.at[st], abuf.at[st], ass.at[s - 1], ars.at[s - 1], device_id={"state": lax.rem(st + s, ns)})

    for it in range(ITERS):
        last = it == ITERS - 1
        for h in range(nh):
            update(it, h)
        for h in range(nh):
            finish(it, h)
            if last and h == 0:
                abuf[st] = free_s[:, :LANE]
                for s in range(1, ns):
                    acopy(s).start()
            denominator(it + 1, h, last)
    for s in range(1, ns):
        acopy(s).wait()
    for h in range(nh):
        for s in range(1, np_):
            fcopy(ITERS - 1, h, s).wait_send()
    free_o[...] = free_s[...] - abuf[0][:, 0:1]

    @pl.loop(0, nc)
    def _(c):
        for s in range(1, ns):
            lcopy(c, s).wait()

        @pl.loop(0, per)
        def _(j):
            g = c * per + j
            own_o[g] = sum(lbuf[q, c, 1, j] for q in range(ns)) - join([lbuf[q, c, 0, j] for q in range(ns)])


def solution(mesh):
    ns, np_ = mesh.shape["state"], mesh.shape["samp"]

    def shards(energies, offsets, counts, labels):
        rows, width = energies.shape
        nblk = offsets.shape[1]
        groups = nblk // SUB
        nc = NC
        nh = 1
        gw = width // groups
        nt = rows * 3 // 4
        nv = rows * 7 // 32 if nblk == LANE else 0
        dma = pltpu.SemaphoreType.DMA
        vm = pl.BlockSpec(memory_space=pltpu.VMEM)
        free, own = pl.pallas_call(
            functools.partial(kernel, ns, np_, nc, nh),
            out_shape=(
                jax.ShapeDtypeStruct((1, rows), jnp.float32),
                jax.ShapeDtypeStruct((groups, SUB, LANE), jnp.float32),
            ),
            in_specs=[pl.BlockSpec(memory_space=pl.ANY)] * 4,
            out_specs=(vm, vm),
            scratch_shapes=[
                pltpu.VMEM((groups, SUB, rows, LANE), jnp.bfloat16),
                pltpu.VMEM((groups, nt // LANE, gw, LANE), jnp.bfloat16),
                pltpu.VMEM(offsets.shape, jnp.float32),
                pltpu.VMEM((1, rows), jnp.int32),
                pltpu.VMEM((groups, SUB, LANE), jnp.int32),
                pltpu.VMEM((groups, SUB, rows), jnp.float32),
                pltpu.VMEM((groups, SUB, LANE), jnp.float32),
                pltpu.VMEM((ITERS, ns, groups, SUB, LANE), jnp.float32),
                pltpu.VMEM((ns, nc, 2, groups // nc, SUB, LANE), jnp.float32),
                pltpu.VMEM((ITERS, nh, np_, 1, rows // nh), jnp.float32),
                pltpu.VMEM((ns, 1, LANE), jnp.float32),
                pltpu.VMEM((1, rows), jnp.float32),
                pltpu.VMEM((1, rows), jnp.float32),
                pltpu.VMEM((SUB, rows // nh - nv), jnp.float32),
                pltpu.VMEM((SUB, rows // nh - nv), jnp.float32),
                pltpu.VMEM((max(nv, 16), LANE), jnp.float32),
                pltpu.VMEM((groups, SUB, LANE), jnp.float32),
                pltpu.VMEM((groups, SUB, LANE), jnp.float32),
                pltpu.VMEM((groups, SUB, LANE), jnp.float32),
                dma((3,)),
                dma((groups, SUB)),
                dma((ITERS, nc, ns - 1)), dma((ITERS, nc, ns - 1)),
                dma((nc, ns - 1)), dma((nc, ns - 1)),
                dma((ITERS, nh, np_ - 1)), dma((ITERS, nh, np_ - 1)),
                dma((ns - 1,)), dma((ns - 1,)),
            ],
            compiler_params=pltpu.CompilerParams(
                collective_id=0, has_side_effects=True, vmem_limit_bytes=60 * 1024 * 1024),
            name="mbar",
        )(energies, offsets, counts.reshape(1, rows), labels.reshape(groups, SUB, LANE))
        def results(free_i, own_i, free_o, own_o):
            free_o[...] = free_i[...]
            own_o[...] = own_i[...]

        return pl.pallas_call(
            results,
            out_shape=(jax.ShapeDtypeStruct((rows,), jnp.float32), jax.ShapeDtypeStruct((width,), jnp.float32)),
            in_specs=[vm, vm],
            out_specs=(vm, vm),
            name="results",
        )(free.reshape(rows), own.reshape(width))

    return jax.shard_map(
        shards,
        mesh=mesh,
        in_specs=(P("state", "samp"), P("state", "samp"), P("state"), P("samp")),
        out_specs=(P("state"), P("samp")),
        check_vma=False,
    )
```
